32 devices in a mesh: seq: 8 (over z, x), batch: 4 (over y, core).
Axes of the slice: x: 2, y: 2, z: 4, core: 2. Of those that a mesh axis runs over, the one named last changes fastest.
Arguments:
- inputs: bfloat16 [32768, 768], P(('batch', 'seq')), parts along dimension 0, may hold values from -6 to 6
- token_rates: float32 [32768], P(('batch', 'seq')), parts along dimension 0, may hold values from 0.1 to 1
- proj_query: bfloat16 [768, 256], replicated, may hold values from -0.21875 to 0.21875
- proj_key: bfloat16 [768, 256], replicated, may hold values from -0.21875 to 0.21875
- proj_value: bfloat16 [768, 256], replicated, may hold values from -0.21875 to 0.21875
- proj_output: bfloat16 [256, 768], replicated, may hold values from -0.375 to 0.375
- fast_in: float32 [256, 512], replicated, may hold values from -0.375 to 0.375
- fast_up: float32 [256, 512], replicated, may hold values from -0.375 to 0.375
- fast_out: float32 [512, 256], replicated, may hold values from -0.25 to 0.25
- cotangent: bfloat16 [32768, 768], P(('batch', 'seq')), parts along dimension 0, may hold values from -6 to 6
Outputs:
- back_inputs: bfloat16 [32768, 768], P(('batch', 'seq')), parts along dimension 0
- back_rate: float32 [32768], P(('batch', 'seq')), parts along dimension 0
- grad_in: float32 [1024, 512], P('batch'), parts along dimension 0
- grad_up: float32 [1024, 512], P('batch'), parts along dimension 0
- grad_out: float32 [2048, 256], P('batch'), parts along dimension 0
- grad_query: float32 [768, 1024], P('seq', 'batch'), parts along dimension 1
- grad_key: float32 [768, 1024], P('seq', 'batch'), parts along dimension 1
- grad_value: float32 [768, 1024], P('seq', 'batch'), parts along dimension 1
- grad_output: float32 [1024, 768], P('batch', 'seq'), parts along dimension 0
The draws below stay inside these ranges and needn't reach their ends.
There are 4 independent parts, one for each index of `batch`. The reference program is written for one: setup_inputs(seed, part) draws one part's arguments, and reference() takes and returns one part's arrays. A program takes and returns all parts, laid end to end along the dimension named above; an argument that names none is the same for every part. Nothing has to cross between parts.
All inputs are finite; a program needn't handle non-finite values.
Results may differ from the reference program's by a relative error of at most 0.029.
Values may be sent and summed in bfloat16 or wider, within the bound.
A program may use at most 128 MiB of HBM per device.

```python
import math
import jax
import jax.numpy as jnp
from jax import lax

D = 768
H = 256
F = 512
NS_STEPS = 5
TOKENS = 8192


def raised(array, key, source, target, parts, factor):
    owner, partner = [(jnp.arange(array.shape[axis_at]) // (array.shape[axis_at] // parts)).reshape([-1 if axis == axis_at else 1 for axis in range(array.ndim)]) for axis_at in (source, target)]
    chosen = jax.random.permutation(key, parts)[partner]
    strong = (owner == chosen) | (owner == (partner + parts // 2) % parts)
    return jnp.where(strong, factor * array, array)


def shard_levels(stream_key, shape, split, low, largest):
    gain = 1.0
    for position, parts in split:
        steps = jax.random.uniform(jax.random.fold_in(jax.random.fold_in(stream_key, 6), position), (parts,), jnp.float32, low / len(split), largest / len(split))
        gain = gain * jnp.repeat(jnp.exp(steps), shape[position] // parts).reshape((-1,) + (1,) * (len(shape) - 1 - position))
    return gain


def gaussian(stream_key, dims, width, limit, cuts=(), held_as=jnp.bfloat16):
    array = width * jax.random.normal(stream_key, dims, jnp.float32)
    if cuts:
        array = array * shard_levels(stream_key, dims, cuts, -0.22, 0.18)
    return jnp.clip(array, -limit, limit).astype(held_as)


def bell_draw_with(key, extent, scale, limit, cuts, heavy, kind=jnp.bfloat16):
    drawn = scale * jax.random.normal(key, extent, jnp.float32)
    if cuts:
        drawn = drawn * shard_levels(key, extent, cuts, -0.22, 0.18)
    return jnp.clip(raised(drawn, jax.random.fold_in(key, 3), *heavy), -limit, limit).astype(kind)


def setup_inputs(seed: int = 0, part: int = 0) -> dict:
    key_list = jax.random.split(jax.random.key(seed), 11)
    part_keys = jax.random.split(jax.random.fold_in(key_list[10], part), 11)
    return {
        "inputs": bell_draw_with(part_keys[0], (TOKENS, D), 1.0, 6.0, ((0, 8),), (0, 1, 8, 2.0)),
        "token_rates": jnp.clip(jnp.exp(math.log(1.0) - 2.3025851 * jax.random.uniform(part_keys[1], (TOKENS,), jnp.float32) ** shard_levels(part_keys[1], (TOKENS,), ((0, 8),), -0.2, 0.2)), 0.1, 1.0),
        "proj_query": gaussian(key_list[2], (D, H), D ** -0.5, 0.21875),
        "proj_key": gaussian(key_list[3], (D, H), D ** -0.5, 0.21875),
        "proj_value": gaussian(key_list[4], (D, H), D ** -0.5, 0.21875),
        "proj_output": gaussian(key_list[5], (H, D), H ** -0.5, 0.375),
        "fast_in": gaussian(key_list[6], (H, F), H ** -0.5, 0.375, (), jnp.float32),
        "fast_up": gaussian(key_list[7], (H, F), H ** -0.5, 0.375, (), jnp.float32),
        "fast_out": gaussian(key_list[8], (F, H), F ** -0.5, 0.25, (), jnp.float32),
        "cotangent": bell_draw_with(part_keys[9], (TOKENS, D), 1.0, 6.0, ((0, 8),), (0, 1, 8, 2.0)),
    }


def rounded(value):
    return value.astype(jnp.bfloat16)

def product(left, right):
    return jnp.dot(left, right, preferred_element_type=jnp.float32)

def token_sum(left, right):
    return lax.dot_general(left, right, (((0,), (0,)), ((), ())), preferred_element_type=jnp.float32)

def times_transpose(left, right):
    return lax.dot_general(left, right, (((1,), (1,)), ((), ())), preferred_element_type=jnp.float32)

def silu_parts(pre_act):
    sigma_val = jax.nn.sigmoid(pre_act)
    activation = pre_act * sigma_val
    slope_val = sigma_val * (1.0 + pre_act * (1.0 - sigma_val))
    curvature = sigma_val * (1.0 - sigma_val) * (2.0 + pre_act * (1.0 - 2.0 * sigma_val))
    return (activation, slope_val, curvature)

def orthogonalize(matrix):
    highest = lax.Precision.HIGHEST
    current = matrix / (jnp.sqrt(jnp.sum(matrix * matrix)) + 1e-07)
    for sweep in range(NS_STEPS):
        gramian = jnp.dot(current, current.T, precision=highest)
        polynom = -4.775 * gramian + 2.0315 * jnp.dot(gramian, gramian, precision=highest)
        current = 3.4445 * current + jnp.dot(polynom, current, precision=highest)
    return current

def project(inputs, proj_query, proj_key, proj_value):
    return (rounded(product(inputs, proj_query)), rounded(product(inputs, proj_key)), rounded(product(inputs, proj_value)))

def update_section(key_rows, value_rows, token_rates, fast_in, fast_up, fast_out):
    w_in, w_up, w_out = (rounded(fast_in), rounded(fast_up), rounded(fast_out))
    scaled = rounded(token_rates[:, None] * value_rows.astype(jnp.float32))
    pre_in = product(key_rows, w_in)
    pre_up = product(key_rows, w_up)
    activation, slope_val, curvature = silu_parts(pre_in)
    hidden = rounded(activation * pre_up)
    upstream = times_transpose(scaled, w_out)
    grad_in_rows = rounded(upstream * pre_up * slope_val)
    grad_up_rows = rounded(upstream * activation)
    partial_value = jnp.stack([token_sum(key_rows, grad_in_rows), token_sum(key_rows, grad_up_rows), token_sum(scaled, hidden)])
    saved = (w_in, w_up, w_out, scaled, pre_in, pre_up, hidden, upstream, grad_in_rows, grad_up_rows)
    return (partial_value, saved)

def query_section(query_rows, cotangent, proj_output, new_in, new_up, new_out):
    n_in, n_up, n_out = (rounded(new_in), rounded(new_up), rounded(new_out))
    pre_p = product(query_rows, n_in)
    pre_r = product(query_rows, n_up)
    activation_q, slope_q, unused_curve = silu_parts(pre_p)
    hidden_q = rounded(activation_q * pre_r)
    output_rows = rounded(product(hidden_q, n_out))
    back_output = rounded(times_transpose(cotangent, proj_output))
    back_hidden = times_transpose(back_output, n_out)
    back_p = rounded(back_hidden * pre_r * slope_q)
    back_r = rounded(back_hidden * activation_q)
    partial_value = jnp.stack([token_sum(query_rows, back_p), token_sum(query_rows, back_r), token_sum(back_output, hidden_q)])
    query_grad = rounded(times_transpose(back_p, n_in) + times_transpose(back_r, n_up))
    return (partial_value, query_grad, output_rows)

def update_backward(saved, key_rows, value_rows, token_rates, back_totals):
    w_in, w_up, w_out, scaled, pre_in, pre_up, hidden, upstream, grad_in_rows, grad_up_rows = saved
    activation, slope_val, curvature = silu_parts(pre_in)
    b_in = rounded(back_totals[0])
    b_up = rounded(back_totals[1])
    b_out = rounded(back_totals[2])
    press_in = product(key_rows, b_in)
    press_up = product(key_rows, b_up)
    back_hid = product(scaled, b_out)
    back_upstream = rounded(press_in * pre_up * slope_val + press_up * activation)
    back_pre_up = rounded(press_in * upstream * slope_val + back_hid * activation)
    back_pre_in = rounded(press_in * upstream * pre_up * curvature + press_up * upstream * slope_val + back_hid * pre_up * slope_val)
    back_scaled = times_transpose(hidden, b_out) + product(back_upstream, w_out)
    back_rate = lax.optimization_barrier(jnp.sum(back_scaled * value_rows.astype(jnp.float32), axis=1))
    contrib = (token_sum(key_rows, back_pre_in), token_sum(key_rows, back_pre_up), token_sum(back_upstream, scaled))
    key_sum = times_transpose(grad_in_rows, b_in) + times_transpose(grad_up_rows, b_up)
    key_sum = key_sum + times_transpose(back_pre_in, w_in) + times_transpose(back_pre_up, w_up)
    key_grad = rounded(key_sum)
    value_grad = rounded(token_rates[:, None] * back_scaled)
    return (contrib, key_grad, value_grad, back_rate)

def input_back(query_grad, key_grad, value_grad, proj_query, proj_key, proj_value):
    total = times_transpose(query_grad, proj_query) + times_transpose(key_grad, proj_key)
    return rounded(total + times_transpose(value_grad, proj_value))

def reference(inputs, token_rates, proj_query, proj_key, proj_value, proj_output, fast_in, fast_up, fast_out, cotangent):
    query_rows, key_rows, value_rows = project(inputs, proj_query, proj_key, proj_value)
    totals, saved = update_section(key_rows, value_rows, token_rates, fast_in, fast_up, fast_out)
    ortho, ns_back = jax.vjp(jax.vmap(orthogonalize), totals)
    new_in = fast_in + ortho[0]
    new_up = fast_up + ortho[1]
    new_out = fast_out + ortho[2].T
    adjoint, query_grad, output_rows = query_section(query_rows, cotangent, proj_output, new_in, new_up, new_out)
    back_totals = ns_back(adjoint)[0]
    contrib, key_grad, value_grad, back_rate = update_backward(saved, key_rows, value_rows, token_rates, back_totals)
    grad_in = adjoint[0] + contrib[0]
    grad_up = adjoint[1] + contrib[1]
    grad_out = adjoint[2].T + contrib[2]
    back_inputs = input_back(query_grad, key_grad, value_grad, proj_query, proj_key, proj_value)
    grad_query = token_sum(inputs, query_grad)
    grad_key = token_sum(inputs, key_grad)
    grad_value = token_sum(inputs, value_grad)
    grad_output = token_sum(output_rows, cotangent)
    return (back_inputs, back_rate, grad_in, grad_up, grad_out, grad_query, grad_key, grad_value, grad_output)
```

```python
import functools

import jax
import jax.numpy as jnp
from jax import lax
from jax.experimental import pallas as pl
from jax.experimental.pallas import tpu as pltpu
from jax.sharding import PartitionSpec as P

NS_STEPS = 5
C1, C3, C5 = 3.4445, -4.775, 2.0315
EPS = 1e-07
MESH = pl.DeviceIdType.MESH
VMEM_LIMIT = 60 * 1024 * 1024
PASSES_FWD = 3
PASSES_BWD = 3


def rounded(value):
    return value.astype(jnp.bfloat16)


def product(left, right):
    return jnp.dot(left, right, preferred_element_type=jnp.float32)


def token_sum(left, right):
    return lax.dot_general(
        left, right, (((0,), (0,)), ((), ())), preferred_element_type=jnp.float32
    )


def times_transpose(left, right):
    return lax.dot_general(
        left, right, (((1,), (1,)), ((), ())), preferred_element_type=jnp.float32
    )


def silu_parts(pre_act):
    sigma_val = jax.nn.sigmoid(pre_act)
    activation = pre_act * sigma_val
    slope_val = sigma_val * (1.0 + pre_act * (1.0 - sigma_val))
    curvature = sigma_val * (1.0 - sigma_val) * (2.0 + pre_act * (1.0 - 2.0 * sigma_val))
    return (activation, slope_val, curvature)


def split(value):
    high = rounded(value)
    return (high, rounded(value - high.astype(jnp.float32)))


def dot_split(left, right, passes, dot):
    if passes == 1:
        return dot(left[0], right[0])
    return dot(left[0], right[0]) + (dot(left[0], right[1]) + dot(left[1], right[0]))


def ns_forward(totals, xs, grams, polys, count, passes):
    norms = []
    for m in range(count):
        norm = jnp.sqrt(jnp.sum(totals[m] * totals[m]))
        norms.append(norm)
        xs[0, m] = totals[m] / (norm + EPS)

    def step(k, carry):
        for m in range(count):
            current = xs[k, m]
            parts = split(current)
            gram = dot_split(parts, parts, passes, times_transpose)
            gparts = split(gram)
            poly = C3 * gram + C5 * dot_split(gparts, gparts, passes, product)
            if grams is not None:
                grams[k, m] = gram
                polys[k, m] = poly
            xs[k + 1, m] = C1 * current + dot_split(split(poly), parts, passes, product)
        return carry

    lax.fori_loop(0, NS_STEPS, step, 0)
    return norms


def ns_backward(totals, norms, xs, grams, polys, grads, count, passes):
    def step(i, carry):
        k = NS_STEPS - 1 - i
        for m in range(count):
            grad = grads[m]
            gparts = split(grad)
            xparts = split(xs[k, m])
            dpoly = dot_split(gparts, xparts, passes, times_transpose)
            sym = dpoly + dpoly.T
            twist = dot_split(split(sym), split(grams[k, m]), passes, product)
            weight = C3 * sym + C5 * (twist + twist.T)
            grads[m] = (
                C1 * grad
                + dot_split(split(polys[k, m]), gparts, passes, product)
                + dot_split(split(weight), xparts, passes, product)
            )
        return carry

    lax.fori_loop(0, NS_STEPS, step, 0)
    out = []
    for m in range(count):
        shifted = norms[m] + EPS
        dot_all = jnp.sum(grads[m] * totals[m])
        out.append(grads[m] / shifted - totals[m] * (dot_all / (norms[m] * shifted * shifted)))
    return out


def greet(n):
    me = lax.axis_index("seq")
    barrier = pltpu.get_barrier_semaphore()
    for d in range(1, n):
        pl.semaphore_signal(
            barrier, inc=1, device_id={"seq": lax.rem(me + d, n)}, device_id_type=MESH
        )
    pl.semaphore_wait(barrier, n - 1)


def start_scatter(n, src, landed, send, recv):
    me = lax.axis_index("seq")
    copies = []
    for d in range(1, n):
        peer = lax.rem(me + d, n)
        copy = pltpu.make_async_remote_copy(
            src_ref=src.at[peer],
            dst_ref=landed.at[d - 1],
            send_sem=send.at[d - 1],
            recv_sem=recv.at[d - 1],
            device_id={"seq": peer},
            device_id_type=MESH,
        )
        copy.start()
        copies.append(copy)
    return copies


def finish_scatter(src, landed, copies):
    total = src[lax.axis_index("seq")].astype(jnp.float32)
    for i, copy in enumerate(copies):
        copy.wait()
        total = total + landed[i].astype(jnp.float32)
    return total


def start_gather(n, mine, gathered, send, recv):
    me = lax.axis_index("seq")
    copies = []
    for d in range(1, n):
        copy = pltpu.make_async_remote_copy(
            src_ref=mine,
            dst_ref=gathered.at[d - 1],
            send_sem=send.at[d - 1],
            recv_sem=recv.at[d - 1],
            device_id={"seq": lax.rem(me + d, n)},
            device_id_type=MESH,
        )
        copy.start()
        copies.append(copy)
    return copies


def finish_gather(n, mine, gathered, copies, full):
    me = lax.axis_index("seq")
    rows = mine.shape[0]
    full[pl.ds(pl.multiple_of(me * rows, rows), rows), :] = mine[...].astype(jnp.float32)
    for d in range(1, n):
        copies[d - 1].wait()
        owner = lax.rem(me - d + n, n)
        full[pl.ds(pl.multiple_of(owner * rows, rows), rows), :] = gathered[d - 1].astype(
            jnp.float32
        )


def forward_kernel(
    n, count, part, fast_in, fast_up, fast_out, n_in, n_up, n_out, total_out,
    landed, mine, gathered, xs, s1, r1, s2, r2,
):
    greet(n)
    copies = start_scatter(n, part, landed, s1, r1)
    mine[...] = rounded(finish_scatter(part, landed, copies))
    copies = start_gather(n, mine, gathered, s2, r2)
    finish_gather(n, mine, gathered, copies, total_out)
    h = total_out.shape[0] // count
    totals = [total_out[m * h : (m + 1) * h, :] for m in range(count)]
    ns_forward(totals, xs, None, None, count, PASSES_FWD)
    n_in[...] = rounded(fast_in[...] + xs[NS_STEPS, 0])
    n_up[...] = rounded(fast_up[...] + xs[NS_STEPS, 1])
    n_out[...] = rounded(fast_out[...] + xs[NS_STEPS, 2].T)


def backward_kernel(
    n, count, part, rows_part, total_ref, adjoint_out, back_out, rows_out,
    landed, mine, gathered, landed_rows, xs, grams, polys, grads, s1, r1, s2, r2, s3, r3,
):
    greet(n)
    copies = start_scatter(n, part, landed, s1, r1)
    h = total_ref.shape[0] // count
    totals = [total_ref[m * h : (m + 1) * h, :] for m in range(count)]
    norms = ns_forward(totals, xs, grams, polys, count, PASSES_FWD)
    mine[...] = rounded(finish_scatter(part, landed, copies))
    copies = start_gather(n, mine, gathered, s2, r2)
    finish_gather(n, mine, gathered, copies, adjoint_out)
    row_copies = start_scatter(n, rows_part, landed_rows, s3, r3)
    for m in range(count):
        grads[m] = adjoint_out[m * h : (m + 1) * h, :]
    result = ns_backward(totals, norms, xs, grams, polys, grads, count, PASSES_BWD)
    for m in range(count):
        back_out[m * h : (m + 1) * h, :] = rounded(result[m])
    rows_out[...] = finish_scatter(rows_part, landed_rows, row_copies)


def final_kernel(
    n, part, rows_part, sum_out, rows_out,
    landed, mine, gathered, landed_rows, s1, r1, s2, r2, s3, r3,
):
    greet(n)
    copies = start_scatter(n, part, landed, s1, r1)
    row_copies = start_scatter(n, rows_part, landed_rows, s3, r3)
    mine[...] = rounded(finish_scatter(part, landed, copies))
    copies = start_gather(n, mine, gathered, s2, r2)
    rows_out[...] = finish_scatter(rows_part, landed_rows, row_copies)
    finish_gather(n, mine, gathered, copies, sum_out)


def call(kernel, identity, outs, scratch, *operands):
    vmem = pl.BlockSpec(memory_space=pltpu.VMEM)
    return pl.pallas_call(
        kernel,
        out_shape=[jax.ShapeDtypeStruct(s, d) for s, d in outs],
        in_specs=[vmem] * len(operands),
        out_specs=[vmem] * len(outs),
        scratch_shapes=scratch,
        compiler_params=pltpu.CompilerParams(
            collective_id=identity, has_side_effects=True, vmem_limit_bytes=VMEM_LIMIT
        ),
    )(*operands)


def sems(n, count):
    return [pltpu.SemaphoreType.DMA((n - 1,)) for _ in range(count)]


def body(
    n,
    inputs,
    token_rates,
    proj_query,
    proj_key,
    proj_value,
    proj_output,
    fast_in,
    fast_up,
    fast_out,
    cotangent,
):
    bf16, f32 = jnp.bfloat16, jnp.float32
    h, f = fast_in.shape
    width = inputs.shape[1]
    count = 3
    block = (count * h // n, f)
    row_block = (width // n, 2 * h)

    query_rows = rounded(product(inputs, proj_query))
    key_rows = rounded(product(inputs, proj_key))
    value_rows = rounded(product(inputs, proj_value))
    w_in, w_up, w_out = (rounded(fast_in), rounded(fast_up), rounded(fast_out))
    scaled = rounded(token_rates[:, None] * value_rows.astype(f32))
    pre_in = product(key_rows, w_in)
    pre_up = product(key_rows, w_up)
    activation, slope_val, curvature = silu_parts(pre_in)
    hidden = rounded(activation * pre_up)
    upstream = times_transpose(scaled, w_out)
    grad_in_rows = rounded(upstream * pre_up * slope_val)
    grad_up_rows = rounded(upstream * activation)

    def stacked(*terms):
        return jnp.concatenate([rounded(t) for t in terms]).reshape((n,) + block)

    def row_stacked(left, right):
        return jnp.concatenate([rounded(left), rounded(right)], axis=1).reshape((n,) + row_block)

    part = stacked(
        token_sum(key_rows, grad_in_rows),
        token_sum(key_rows, grad_up_rows),
        token_sum(scaled, hidden),
    )
    exchange = [
        pltpu.VMEM((n - 1,) + block, bf16),
        pltpu.VMEM(block, bf16),
        pltpu.VMEM((n - 1,) + block, bf16),
    ]
    n_in, n_up, n_out, totals = call(
        functools.partial(forward_kernel, n, count),
        0,
        [((h, f), bf16), ((h, f), bf16), ((f, h), bf16), ((count * h, f), f32)],
        exchange + [pltpu.VMEM((NS_STEPS + 1, count, h, f), f32)] + sems(n, 4),
        part, fast_in, fast_up, fast_out,
    )

    pre_p = product(query_rows, n_in)
    pre_r = product(query_rows, n_up)
    activation_q, slope_q, _ = silu_parts(pre_p)
    hidden_q = rounded(activation_q * pre_r)
    output_rows = rounded(product(hidden_q, n_out))
    back_output = rounded(times_transpose(cotangent, proj_output))
    back_hidden = times_transpose(back_output, n_out)
    back_p = rounded(back_hidden * pre_r * slope_q)
    back_r = rounded(back_hidden * activation_q)
    query_grad = rounded(times_transpose(back_p, n_in) + times_transpose(back_r, n_up))
    part = stacked(
        token_sum(query_rows, back_p),
        token_sum(query_rows, back_r),
        token_sum(back_output, hidden_q),
    )
    rows_part = row_stacked(token_sum(inputs, query_grad), token_sum(cotangent, output_rows))
    row_scratch = [pltpu.VMEM((n - 1,) + row_block, bf16)]
    adjoint, back_totals, rows_sum = call(
        functools.partial(backward_kernel, n, count),
        1,
        [((count * h, f), f32), ((count * h, f), bf16), (row_block, f32)],
        exchange
        + row_scratch
        + [
            pltpu.VMEM((NS_STEPS + 1, count, h, f), f32),
            pltpu.VMEM((NS_STEPS, count, h, h), f32),
            pltpu.VMEM((NS_STEPS, count, h, h), f32),
            pltpu.VMEM((count, h, f), f32),
        ]
        + sems(n, 6),
        part, rows_part, totals,
    )
    grad_query = rows_sum[:, :h]
    grad_output = rows_sum[:, h:].T

    b_in, b_up, b_out = (back_totals[m * h : (m + 1) * h] for m in range(count))
    press_in = product(key_rows, b_in)
    press_up = product(key_rows, b_up)
    back_hid = product(scaled, b_out)
    back_upstream = rounded(press_in * pre_up * slope_val + press_up * activation)
    back_pre_up = rounded(press_in * upstream * slope_val + back_hid * activation)
    back_pre_in = rounded(
        press_in * upstream * pre_up * curvature
        + press_up * upstream * slope_val
        + back_hid * pre_up * slope_val
    )
    back_scaled = times_transpose(hidden, b_out) + product(back_upstream, w_out)
    back_rate = jnp.sum(back_scaled * value_rows.astype(f32), axis=1)
    key_sum = times_transpose(grad_in_rows, b_in) + times_transpose(grad_up_rows, b_up)
    key_sum = key_sum + times_transpose(back_pre_in, w_in) + times_transpose(back_pre_up, w_up)
    key_grad = rounded(key_sum)
    value_grad = rounded(token_rates[:, None] * back_scaled)
    part = stacked(
        token_sum(key_rows, back_pre_in),
        token_sum(key_rows, back_pre_up),
        token_sum(scaled, back_upstream),
    )
    rows_part = row_stacked(token_sum(inputs, key_grad), token_sum(inputs, value_grad))
    summed, rows_sum = call(
        functools.partial(final_kernel, n),
        2,
        [((count * h, f), f32), (row_block, f32)],
        exchange + row_scratch + sems(n, 6),
        part, rows_part,
    )
    grad_key = rows_sum[:, :h]
    grad_value = rows_sum[:, h:]
    both = adjoint + summed
    grad_in = both[:h]
    grad_up = both[h : 2 * h]
    grad_out = both[2 * h :].T
    total = times_transpose(query_grad, proj_query) + times_transpose(key_grad, proj_key)
    back_inputs = rounded(total + times_transpose(value_grad, proj_value))
    return (
        back_inputs,
        back_rate,
        grad_in,
        grad_up,
        grad_out,
        grad_query,
        grad_key,
        grad_value,
        grad_output,
    )


def solution(mesh):
    in_specs = (
        P(("batch", "seq"), None),
        P(("batch", "seq")),
        P(),
        P(),
        P(),
        P(),
        P(),
        P(),
        P(),
        P(("batch", "seq"), None),
    )
    out_specs = (
        P(("batch", "seq"), None),
        P(("batch", "seq")),
        P("batch", None),
        P("batch", None),
        P("batch", None),
        P("seq", "batch"),
        P("seq", "batch"),
        P("seq", "batch"),
        P("batch", "seq"),
    )
    return jax.shard_map(
        functools.partial(body, mesh.shape["seq"]),
        mesh=mesh,
        in_specs=in_specs,
        out_specs=out_specs,
        check_vma=False,
    )
```

```python
import functools

import jax
import jax.numpy as jnp
from jax import lax
from jax.experimental import pallas as pl
from jax.experimental.pallas import tpu as pltpu
from jax.sharding import PartitionSpec as P

NS_STEPS = 5
C1, C3, C5 = 3.4445, -4.775, 2.0315
EPS = 1e-07
MESH = pl.DeviceIdType.MESH
VMEM_LIMIT = 60 * 1024 * 1024
PAIR = 2
PASSES_FWD = 3
PASSES_BWD = 3


def rounded(value):
    return value.astype(jnp.bfloat16)


def product(left, right):
    return jnp.dot(left, right, preferred_element_type=jnp.float32)


def token_sum(left, right):
    return lax.dot_general(
        left, right, (((0,), (0,)), ((), ())), preferred_element_type=jnp.float32
    )


def times_transpose(left, right):
    return lax.dot_general(
        left, right, (((1,), (1,)), ((), ())), preferred_element_type=jnp.float32
    )


def silu_parts(pre_act):
    sigma_val = jax.nn.sigmoid(pre_act)
    activation = pre_act * sigma_val
    slope_val = sigma_val * (1.0 + pre_act * (1.0 - sigma_val))
    curvature = sigma_val * (1.0 - sigma_val) * (2.0 + pre_act * (1.0 - 2.0 * sigma_val))
    return (activation, slope_val, curvature)


def split(value, passes):
    high = rounded(value)
    if passes == 1:
        return (high,)
    return (high, rounded(value - high.astype(jnp.float32)))


def dot_split(left, right, dot):
    if len(left) == 1:
        return dot(left[0], right[0])
    along = 1 if dot is times_transpose else 0
    return dot(
        jnp.concatenate([left[0], left[0], left[1]], axis=1),
        jnp.concatenate([right[0], right[1], right[0]], axis=along),
    )


def ns_start(totals, xs):
    norms = []
    for m, matrix in enumerate(totals):
        norm = jnp.sqrt(jnp.sum(matrix * matrix))
        norms.append(norm)
        xs[0, m] = matrix / (norm + EPS)
    return norms


def ns_forward(first, last, xs, grams, polys, count, passes):
    each = range(count)

    def step(k, carry):
        xparts = [split(xs[k, m], passes) for m in each]
        gram = [dot_split(xparts[m], xparts[m], times_transpose) for m in each]
        gparts = [split(gram[m], passes) for m in each]
        poly = [C3 * gram[m] + C5 * dot_split(gparts[m], gparts[m], product) for m in each]
        pparts = [split(poly[m], passes) for m in each]
        for m in each:
            if grams is not None:
                grams[k, m] = gram[m]
                polys[k, m] = poly[m]
            xs[k + 1, m] = C1 * xs[k, m] + dot_split(pparts[m], xparts[m], product)
        return carry

    lax.fori_loop(first, last, step, 0)


def ns_backward(totals, norms, xs, grams, polys, grads, count, passes):
    each = range(count)

    def step(i, carry):
        k = NS_STEPS - 1 - i
        gparts = [split(grads[m], passes) for m in each]
        xparts = [split(xs[k, m], passes) for m in each]
        dpoly = [dot_split(gparts[m], xparts[m], times_transpose) for m in each]
        sym = [dpoly[m] + dpoly[m].T for m in each]
        twist = [
            dot_split(split(sym[m], passes), split(grams[k, m], passes), product) for m in each
        ]
        weight = [C3 * sym[m] + C5 * (twist[m] + twist[m].T) for m in each]
        for m in each:
            grads[m] = (
                C1 * grads[m]
                + dot_split(split(polys[k, m], passes), gparts[m], product)
                + dot_split(split(weight[m], passes), xparts[m], product)
            )
        return carry

    lax.fori_loop(0, NS_STEPS, step, 0)
    out = []
    for m in each:
        shifted = norms[m] + EPS
        dot_all = jnp.sum(grads[m] * totals[m])
        out.append(grads[m] / shifted - totals[m] * (dot_all / (norms[m] * shifted * shifted)))
    return out


def place():
    me = lax.axis_index("seq")
    return me // PAIR, me % PAIR


def remote(src, dst, send, recv, device):
    copy = pltpu.make_async_remote_copy(
        src_ref=src,
        dst_ref=dst,
        send_sem=send,
        recv_sem=recv,
        device_id={"seq": device},
        device_id_type=MESH,
    )
    copy.start()
    return copy


def line_peer(lines, d):
    line, side = place()
    return lax.rem(line + d, lines) * PAIR + side


def partner():
    line, side = place()
    return line * PAIR + (1 - side)


def greet(lines):
    barrier = pltpu.get_barrier_semaphore()
    for peer in [partner()] + [line_peer(lines, d) for d in range(1, lines)]:
        pl.semaphore_signal(barrier, inc=1, device_id={"seq": peer}, device_id_type=MESH)
    pl.semaphore_wait(barrier, lines)


def start_pairs(lines, src, buf):
    line, side = place()
    copies = []
    for d in list(range(1, lines)) + [0]:
        to = lax.rem(line + d, lines)
        copies.append(
            remote(
                src.at[to * PAIR + (1 - side)],
                buf.paired.at[d],
                buf.sems.at[0, d],
                buf.sems.at[1, d],
                partner(),
            )
        )
    return copies


def forward_pairs(lines, src, buf, copies):
    line, side = place()
    sent = []
    for d, copy in zip(range(1, lines), copies):
        to = lax.rem(line + d, lines)
        copy.wait()
        buf.middle[d] = rounded(
            src[to * PAIR + side].astype(jnp.float32) + buf.paired[d].astype(jnp.float32)
        )
        sent.append(
            remote(
                buf.middle.at[d],
                buf.lined.at[d],
                buf.sems.at[2, d],
                buf.sems.at[3, d],
                to * PAIR + side,
            )
        )
    return sent


def finish_scatter(lines, src, buf, copies, sent):
    copies[-1].wait()
    total = src[lax.axis_index("seq")].astype(jnp.float32) + buf.paired[0].astype(jnp.float32)
    for d, copy in zip(range(1, lines), sent):
        copy.wait()
        total = total + buf.lined[d].astype(jnp.float32)
    return total


def start_gather(lines, buf):
    out = []
    for d in range(1, lines):
        out.append(
            remote(
                buf.mine,
                buf.gathered.at[d],
                buf.sems.at[4, d],
                buf.sems.at[5, d],
                line_peer(lines, d),
            )
        )
    across = remote(buf.mine, buf.crossed.at[0], buf.sems.at[6, 0], buf.sems.at[7, 0], partner())
    return out, [across]


def finish_gather(lines, buf, copies, full):
    line, side = place()
    rows = buf.mine.shape[0]
    out, across = copies

    def put(owner, block):
        full[pl.ds(pl.multiple_of(owner * rows, rows), rows), :] = block.astype(jnp.float32)

    for d in range(1, lines):
        out[d - 1].wait()
        across.append(
            remote(
                buf.gathered.at[d],
                buf.crossed.at[d],
                buf.sems.at[6, d],
                buf.sems.at[7, d],
                partner(),
            )
        )
    put(line * PAIR + side, buf.mine[...])
    for d in range(1, lines):
        put(lax.rem(line - d + lines, lines) * PAIR + side, buf.gathered[d])
    for d in range(lines):
        across[d].wait()
        put(lax.rem(line - d + lines, lines) * PAIR + (1 - side), buf.crossed[d])


class Scatter:
    def __init__(self, paired, middle, lined, sems):
        self.paired, self.middle, self.lined, self.sems = paired, middle, lined, sems

    @staticmethod
    def scratch(lines, block):
        slots = pltpu.VMEM((lines,) + block, jnp.bfloat16)
        return [slots, slots, slots, pltpu.SemaphoreType.DMA((4, lines))]


class Reduce(Scatter):
    def __init__(self, paired, middle, lined, mine, gathered, crossed, sems):
        super().__init__(paired, middle, lined, sems)
        self.mine, self.gathered, self.crossed = mine, gathered, crossed

    @staticmethod
    def scratch(lines, block):
        slots = pltpu.VMEM((lines,) + block, jnp.bfloat16)
        one = pltpu.VMEM(block, jnp.bfloat16)
        return [slots, slots, slots, one, slots, slots, pltpu.SemaphoreType.DMA((8, lines))]


def forward_kernel(
    lines, count, part, fast_in, fast_up, fast_out, n_in, n_up, n_out, total_out, *scratch
):
    buf, xs = Reduce(*scratch[:7]), scratch[7]
    greet(lines)
    copies = start_pairs(lines, part, buf)
    sent = forward_pairs(lines, part, buf, copies)
    buf.mine[...] = rounded(finish_scatter(lines, part, buf, copies, sent))
    finish_gather(lines, buf, start_gather(lines, buf), total_out)
    h = total_out.shape[0] // count
    totals = [total_out[m * h : (m + 1) * h, :] for m in range(count)]
    ns_start(totals, xs)
    ns_forward(0, NS_STEPS, xs, None, None, count, PASSES_FWD)
    n_in[...] = rounded(fast_in[...] + xs[NS_STEPS, 0])
    n_up[...] = rounded(fast_up[...] + xs[NS_STEPS, 1])
    n_out[...] = rounded(fast_out[...] + xs[NS_STEPS, 2].T)


def backward_kernel(
    lines, count, part, rows_part, total_ref, adjoint_out, back_out, rows_out, *scratch
):
    buf, row_buf = Reduce(*scratch[:7]), Scatter(*scratch[7:11])
    xs, grams, polys, grads = scratch[11:]
    greet(lines)
    copies = start_pairs(lines, part, buf)
    h = total_ref.shape[0] // count
    totals = [total_ref[m * h : (m + 1) * h, :] for m in range(count)]
    norms = ns_start(totals, xs)
    ns_forward(0, NS_STEPS - 4, xs, grams, polys, count, PASSES_FWD)
    sent = forward_pairs(lines, part, buf, copies)
    ns_forward(NS_STEPS - 4, NS_STEPS - 2, xs, grams, polys, count, PASSES_FWD)
    buf.mine[...] = rounded(finish_scatter(lines, part, buf, copies, sent))
    gathering = start_gather(lines, buf)
    ns_forward(NS_STEPS - 2, NS_STEPS, xs, grams, polys, count, PASSES_FWD)
    finish_gather(lines, buf, gathering, adjoint_out)
    copies = start_pairs(lines, rows_part, row_buf)
    sent = forward_pairs(lines, rows_part, row_buf, copies)
    for m in range(count):
        grads[m] = adjoint_out[m * h : (m + 1) * h, :]
    result = ns_backward(totals, norms, xs, grams, polys, grads, count, PASSES_BWD)
    for m in range(count):
        back_out[m * h : (m + 1) * h, :] = rounded(result[m])
    rows_out[...] = finish_scatter(lines, rows_part, row_buf, copies, sent)


def final_kernel(lines, part, rows_part, sum_out, rows_out, *scratch):
    buf, row_buf = Reduce(*scratch[:7]), Scatter(*scratch[7:11])
    greet(lines)
    copies = start_pairs(lines, part, buf)
    row_copies = start_pairs(lines, rows_part, row_buf)
    sent = forward_pairs(lines, part, buf, copies)
    buf.mine[...] = rounded(finish_scatter(lines, part, buf, copies, sent))
    row_sent = forward_pairs(lines, rows_part, row_buf, row_copies)
    gathering = start_gather(lines, buf)
    rows_out[...] = finish_scatter(lines, rows_part, row_buf, row_copies, row_sent)
    finish_gather(lines, buf, gathering, sum_out)


def call(kernel, identity, outs, scratch, *operands):
    vmem = pl.BlockSpec(memory_space=pltpu.VMEM)
    return pl.pallas_call(
        kernel,
        out_shape=[jax.ShapeDtypeStruct(s, d) for s, d in outs],
        in_specs=[vmem] * len(operands),
        out_specs=[vmem] * len(outs),
        scratch_shapes=scratch,
        compiler_params=pltpu.CompilerParams(
            collective_id=identity, has_side_effects=True, vmem_limit_bytes=VMEM_LIMIT
        ),
    )(*operands)


def body(
    n,
    inputs,
    token_rates,
    proj_query,
    proj_key,
    proj_value,
    proj_output,
    fast_in,
    fast_up,
    fast_out,
    cotangent,
):
    bf16, f32 = jnp.bfloat16, jnp.float32
    h, f = fast_in.shape
    width = inputs.shape[1]
    count = 3
    block = (count * h // n, f)
    row_block = (width // n, 2 * h)

    query_rows = rounded(product(inputs, proj_query))
    key_rows = rounded(product(inputs, proj_key))
    value_rows = rounded(product(inputs, proj_value))
    w_in, w_up, w_out = (rounded(fast_in), rounded(fast_up), rounded(fast_out))
    scaled = rounded(token_rates[:, None] * value_rows.astype(f32))
    pre_in = product(key_rows, w_in)
    pre_up = product(key_rows, w_up)
    activation, slope_val, curvature = silu_parts(pre_in)
    hidden = rounded(activation * pre_up)
    upstream = times_transpose(scaled, w_out)
    grad_in_rows = rounded(upstream * pre_up * slope_val)
    grad_up_rows = rounded(upstream * activation)

    def stacked(*terms):
        return jnp.concatenate([rounded(t) for t in terms]).reshape((n,) + block)

    def row_stacked(left, right):
        return jnp.concatenate([rounded(left), rounded(right)], axis=1).reshape((n,) + row_block)

    part = stacked(
        token_sum(key_rows, grad_in_rows),
        token_sum(key_rows, grad_up_rows),
        token_sum(scaled, hidden),
    )
    lines = n // PAIR
    exchange = Reduce.scratch(lines, block)
    row_scratch = Scatter.scratch(lines, row_block)
    n_in, n_up, n_out, totals = call(
        functools.partial(forward_kernel, lines, count),
        0,
        [((h, f), bf16), ((h, f), bf16), ((f, h), bf16), ((count * h, f), f32)],
        exchange + [pltpu.VMEM((NS_STEPS + 1, count, h, f), f32)],
        part, fast_in, fast_up, fast_out,
    )

    pre_p = product(query_rows, n_in)
    pre_r = product(query_rows, n_up)
    activation_q, slope_q, _ = silu_parts(pre_p)
    hidden_q = rounded(activation_q * pre_r)
    output_rows = rounded(product(hidden_q, n_out))
    back_output = rounded(times_transpose(cotangent, proj_output))
    back_hidden = times_transpose(back_output, n_out)
    back_p = rounded(back_hidden * pre_r * slope_q)
    back_r = rounded(back_hidden * activation_q)
    query_grad = rounded(times_transpose(back_p, n_in) + times_transpose(back_r, n_up))
    part = stacked(
        token_sum(query_rows, back_p),
        token_sum(query_rows, back_r),
        token_sum(back_output, hidden_q),
    )
    rows_part = row_stacked(token_sum(inputs, query_grad), token_sum(cotangent, output_rows))
    adjoint, back_totals, rows_sum = call(
        functools.partial(backward_kernel, lines, count),
        1,
        [((count * h, f), f32), ((count * h, f), bf16), (row_block, f32)],
        exchange
        + row_scratch
        + [
            pltpu.VMEM((NS_STEPS + 1, count, h, f), f32),
            pltpu.VMEM((NS_STEPS, count, h, h), f32),
            pltpu.VMEM((NS_STEPS, count, h, h), f32),
            pltpu.VMEM((count, h, f), f32),
        ],
        part, rows_part, totals,
    )
    grad_query = rows_sum[:, :h]
    grad_output = rows_sum[:, h:].T

    b_in, b_up, b_out = (back_totals[m * h : (m + 1) * h] for m in range(count))
    press_in = product(key_rows, b_in)
    press_up = product(key_rows, b_up)
    back_hid = product(scaled, b_out)
    back_upstream = rounded(press_in * pre_up * slope_val + press_up * activation)
    back_pre_up = rounded(press_in * upstream * slope_val + back_hid * activation)
    back_pre_in = rounded(
        press_in * upstream * pre_up * curvature
        + press_up * upstream * slope_val
        + back_hid * pre_up * slope_val
    )
    back_scaled = times_transpose(hidden, b_out) + product(back_upstream, w_out)
    back_rate = jnp.sum(back_scaled * value_rows.astype(f32), axis=1)
    key_sum = times_transpose(grad_in_rows, b_in) + times_transpose(grad_up_rows, b_up)
    key_sum = key_sum + times_transpose(back_pre_in, w_in) + times_transpose(back_pre_up, w_up)
    key_grad = rounded(key_sum)
    value_grad = rounded(token_rates[:, None] * back_scaled)
    part = stacked(
        token_sum(key_rows, back_pre_in),
        token_sum(key_rows, back_pre_up),
        token_sum(scaled, back_upstream),
    )
    rows_part = row_stacked(token_sum(inputs, key_grad), token_sum(inputs, value_grad))
    summed, rows_sum = call(
        functools.partial(final_kernel, lines),
        2,
        [((count * h, f), f32), (row_block, f32)],
        exchange + row_scratch,
        part, rows_part,
    )
    grad_key = rows_sum[:, :h]
    grad_value = rows_sum[:, h:]
    both = adjoint + summed
    grad_in = both[:h]
    grad_up = both[h : 2 * h]
    grad_out = both[2 * h :].T
    total = times_transpose(query_grad, proj_query) + times_transpose(key_grad, proj_key)
    back_inputs = rounded(total + times_transpose(value_grad, proj_value))
    return (
        back_inputs,
        back_rate,
        grad_in,
        grad_up,
        grad_out,
        grad_query,
        grad_key,
        grad_value,
        grad_output,
    )


def solution(mesh):
    in_specs = (
        P(("batch", "seq"), None),
        P(("batch", "seq")),
        P(),
        P(),
        P(),
        P(),
        P(),
        P(),
        P(),
        P(("batch", "seq"), None),
    )
    out_specs = (
        P(("batch", "seq"), None),
        P(("batch", "seq")),
        P("batch", None),
        P("batch", None),
        P("batch", None),
        P("seq", "batch"),
        P("seq", "batch"),
        P("seq", "batch"),
        P("batch", "seq"),
    )
    return jax.shard_map(
        functools.partial(body, mesh.shape["seq"]),
        mesh=mesh,
        in_specs=in_specs,
        out_specs=out_specs,
        check_vma=False,
    )
```

```python
import functools
import math

import jax
import jax.numpy as jnp
from jax import lax
from jax.experimental import pallas as pl
from jax.experimental.pallas import tpu as pltpu
from jax.sharding import PartitionSpec as P

NS_STEPS = 5
C1, C3, C5 = 3.4445, -4.775, 2.0315
EPS = 1e-07
MESH = pl.DeviceIdType.MESH
VMEM_LIMIT = 60 * 1024 * 1024
PAIR = 2
PASSES_FWD = 3
PASSES_BWD = 3


def rounded(value):
    return value.astype(jnp.bfloat16)


def product(left, right):
    return jnp.dot(left, right, preferred_element_type=jnp.float32)


def token_sum(left, right):
    return lax.dot_general(
        left, right, (((0,), (0,)), ((), ())), preferred_element_type=jnp.float32
    )


def times_transpose(left, right):
    return lax.dot_general(
        left, right, (((1,), (1,)), ((), ())), preferred_element_type=jnp.float32
    )


def silu_parts(pre_act):
    sigma_val = jax.nn.sigmoid(pre_act)
    activation = pre_act * sigma_val
    slope_val = sigma_val * (1.0 + pre_act * (1.0 - sigma_val))
    curvature = sigma_val * (1.0 - sigma_val) * (2.0 + pre_act * (1.0 - 2.0 * sigma_val))
    return (activation, slope_val, curvature)


def split(value, passes):
    high = rounded(value)
    if passes == 1:
        return (high,)
    return (high, rounded(value - high.astype(jnp.float32)))


def dot_split(left, right, dot):
    if len(left) == 1:
        return dot(left[0], right[0])
    along = 1 if dot is times_transpose else 0
    return dot(
        jnp.concatenate([left[0], left[0], left[1]], axis=1),
        jnp.concatenate([right[0], right[1], right[0]], axis=along),
    )


def ns_start(totals, xs):
    norms = []
    for m, matrix in enumerate(totals):
        norm = jnp.sqrt(jnp.sum(matrix * matrix))
        norms.append(norm)
        xs[0, m] = matrix / (norm + EPS)
    return norms


def ns_forward(first, last, xs, grams, polys, count, passes):
    each = range(count)

    def step(k, carry):
        xparts = [split(xs[k, m], passes) for m in each]
        gram = [dot_split(xparts[m], xparts[m], times_transpose) for m in each]
        gparts = [split(gram[m], passes) for m in each]
        poly = [C3 * gram[m] + C5 * dot_split(gparts[m], gparts[m], product) for m in each]
        pparts = [split(poly[m], passes) for m in each]
        for m in each:
            if grams is not None:
                grams[k, m] = gram[m]
                polys[k, m] = poly[m]
            xs[k + 1, m] = C1 * xs[k, m] + dot_split(pparts[m], xparts[m], product)
        return carry

    lax.fori_loop(first, last, step, 0)


def ns_backward(first, last, xs, grams, polys, grads, count, passes):
    each = range(count)

    def step(i, carry):
        k = NS_STEPS - 1 - i
        gparts = [split(grads[m], passes) for m in each]
        xparts = [split(xs[k, m], passes) for m in each]
        dpoly = [dot_split(gparts[m], xparts[m], times_transpose) for m in each]
        sym = [dpoly[m] + dpoly[m].T for m in each]
        twist = [
            dot_split(split(sym[m], passes), split(grams[k, m], passes), product) for m in each
        ]
        weight = [C3 * sym[m] + C5 * (twist[m] + twist[m].T) for m in each]
        for m in each:
            grads[m] = (
                C1 * grads[m]
                + dot_split(split(polys[k, m], passes), gparts[m], product)
                + dot_split(split(weight[m], passes), xparts[m], product)
            )
        return carry

    lax.fori_loop(first, last, step, 0)


def ns_finish(totals, norms, grads, count):
    out = []
    for m in range(count):
        shifted = norms[m] + EPS
        dot_all = jnp.sum(grads[m] * totals[m])
        out.append(grads[m] / shifted - totals[m] * (dot_all / (norms[m] * shifted * shifted)))
    return out


def place():
    me = lax.axis_index("seq")
    return me // PAIR, me % PAIR


def remote(src, dst, send, recv, device):
    copy = pltpu.make_async_remote_copy(
        src_ref=src,
        dst_ref=dst,
        send_sem=send,
        recv_sem=recv,
        device_id={"seq": device},
        device_id_type=MESH,
    )
    copy.start()
    return copy


def line_peer(lines, d):
    line, side = place()
    return lax.rem(line + d, lines) * PAIR + side


def partner():
    line, side = place()
    return line * PAIR + (1 - side)


def greet(lines):
    barrier = pltpu.get_barrier_semaphore()
    for peer in [partner()] + [line_peer(lines, d) for d in range(1, lines)]:
        pl.semaphore_signal(barrier, inc=1, device_id={"seq": peer}, device_id_type=MESH)
    pl.semaphore_wait(barrier, lines)


def start_pairs(lines, src, buf):
    line, side = place()
    copies = []
    for d in list(range(1, lines)) + [0]:
        to = lax.rem(line + d, lines)
        copies.append(
            remote(
                src.at[to * PAIR + (1 - side)],
                buf.paired.at[d],
                buf.sems.at[0, d],
                buf.sems.at[1, d],
                partner(),
            )
        )
    return copies


def forward_pairs(lines, src, buf, copies):
    line, side = place()
    sent = []
    for d, copy in zip(range(1, lines), copies):
        to = lax.rem(line + d, lines)
        copy.wait()
        buf.middle[d] = rounded(
            src[to * PAIR + side].astype(jnp.float32) + buf.paired[d].astype(jnp.float32)
        )
        sent.append(
            remote(
                buf.middle.at[d],
                buf.lined.at[d],
                buf.sems.at[2, d],
                buf.sems.at[3, d],
                to * PAIR + side,
            )
        )
    return sent


def finish_scatter(lines, src, buf, copies, sent):
    copies[-1].wait()
    total = src[lax.axis_index("seq")].astype(jnp.float32) + buf.paired[0].astype(jnp.float32)
    for d, copy in zip(range(1, lines), sent):
        copy.wait()
        total = total + buf.lined[d].astype(jnp.float32)
    return total


def start_gather(lines, buf):
    out = []
    for d in range(1, lines):
        out.append(
            remote(
                buf.mine,
                buf.gathered.at[d],
                buf.sems.at[4, d],
                buf.sems.at[5, d],
                line_peer(lines, d),
            )
        )
    across = remote(buf.mine, buf.crossed.at[0], buf.sems.at[6, 0], buf.sems.at[7, 0], partner())
    return out, [across]


def relay_gather(lines, buf, copies):
    out, across = copies
    for d in range(1, lines):
        out[d - 1].wait()
        across.append(
            remote(
                buf.gathered.at[d],
                buf.crossed.at[d],
                buf.sems.at[6, d],
                buf.sems.at[7, d],
                partner(),
            )
        )


def finish_gather(lines, buf, copies, full):
    line, side = place()
    rows = buf.mine.shape[0]
    across = copies[1]

    def put(owner, block):
        full[pl.ds(pl.multiple_of(owner * rows, rows), rows), :] = block.astype(jnp.float32)

    put(line * PAIR + side, buf.mine[...])
    for d in range(1, lines):
        put(lax.rem(line - d + lines, lines) * PAIR + side, buf.gathered[d])
    for d in range(lines):
        across[d].wait()
        put(lax.rem(line - d + lines, lines) * PAIR + (1 - side), buf.crossed[d])


class Scatter:
    def __init__(self, paired, middle, lined, sems):
        self.paired, self.middle, self.lined, self.sems = paired, middle, lined, sems

    @staticmethod
    def scratch(lines, block):
        slots = pltpu.VMEM((lines,) + block, jnp.bfloat16)
        return [slots, slots, slots, pltpu.SemaphoreType.DMA((4, lines))]


class Reduce(Scatter):
    def __init__(self, paired, middle, lined, mine, gathered, crossed, sems):
        super().__init__(paired, middle, lined, sems)
        self.mine, self.gathered, self.crossed = mine, gathered, crossed

    @staticmethod
    def scratch(lines, block):
        slots = pltpu.VMEM((lines,) + block, jnp.bfloat16)
        one = pltpu.VMEM(block, jnp.bfloat16)
        return [slots, slots, slots, one, slots, slots, pltpu.SemaphoreType.DMA((8, lines))]


def forward_kernel(
    lines, count, part, fast_in, fast_up, fast_out, n_in, n_up, n_out, total_out, *scratch
):
    buf, xs = Reduce(*scratch[:7]), scratch[7]
    greet(lines)
    copies = start_pairs(lines, part, buf)
    sent = forward_pairs(lines, part, buf, copies)
    buf.mine[...] = rounded(finish_scatter(lines, part, buf, copies, sent))
    gathering = start_gather(lines, buf)
    relay_gather(lines, buf, gathering)
    finish_gather(lines, buf, gathering, total_out)
    h = total_out.shape[0] // count
    totals = [total_out[m * h : (m + 1) * h, :] for m in range(count)]
    ns_start(totals, xs)
    ns_forward(0, NS_STEPS, xs, None, None, count, PASSES_FWD)
    n_in[...] = rounded(fast_in[...] + xs[NS_STEPS, 0])
    n_up[...] = rounded(fast_up[...] + xs[NS_STEPS, 1])
    n_out[...] = rounded(fast_out[...] + xs[NS_STEPS, 2].T)


def fill_rows(rows_part, pairs):
    n, rows = rows_part.shape[:2]
    at = 0
    for left, right in pairs:
        total = token_sum(left[...], right[...])
        wide = total.shape[1]
        for j in range(n):
            rows_part[j, :, at : at + wide] = rounded(total[j * rows : (j + 1) * rows, :])
        at += wide


def backward_kernel(
    lines, count, part, inputs, query_grad, cotangent, output_rows, total_ref,
    adjoint_out, back_out, rows_out, *scratch
):
    buf, row_buf = Reduce(*scratch[:7]), Scatter(*scratch[7:11])
    rows_part, xs, grams, polys, grads = scratch[11:]
    greet(lines)
    copies = start_pairs(lines, part, buf)
    h = total_ref.shape[0] // count
    totals = [total_ref[m * h : (m + 1) * h, :] for m in range(count)]
    norms = ns_start(totals, xs)
    fill_rows(rows_part, ((inputs, query_grad), (cotangent, output_rows)))
    ns_forward(0, NS_STEPS - 4, xs, grams, polys, count, PASSES_FWD)
    sent = forward_pairs(lines, part, buf, copies)
    ns_forward(NS_STEPS - 4, NS_STEPS - 2, xs, grams, polys, count, PASSES_FWD)
    buf.mine[...] = rounded(finish_scatter(lines, part, buf, copies, sent))
    gathering = start_gather(lines, buf)
    ns_forward(NS_STEPS - 2, NS_STEPS, xs, grams, polys, count, PASSES_FWD)
    relay_gather(lines, buf, gathering)
    finish_gather(lines, buf, gathering, adjoint_out)
    copies = start_pairs(lines, rows_part, row_buf)
    for m in range(count):
        grads[m] = adjoint_out[m * h : (m + 1) * h, :]
    ns_backward(0, NS_STEPS - 2, xs, grams, polys, grads, count, PASSES_BWD)
    sent = forward_pairs(lines, rows_part, row_buf, copies)
    ns_backward(NS_STEPS - 2, NS_STEPS, xs, grams, polys, grads, count, PASSES_BWD)
    result = ns_finish(totals, norms, grads, count)
    for m in range(count):
        back_out[m * h : (m + 1) * h, :] = rounded(result[m])
    rows_out[...] = finish_scatter(lines, rows_part, row_buf, copies, sent)


def final_kernel(
    lines, count, part, inputs, query_grad, key_grad, value_grad,
    proj_query, proj_key, proj_value, adjoint,
    grad_in, grad_up, grad_out, grad_key, grad_value, back_inputs, *scratch
):
    buf, row_buf = Reduce(*scratch[:7]), Scatter(*scratch[7:11])
    rows_part, total = scratch[11:]
    greet(lines)
    copies = start_pairs(lines, part, buf)
    fill_rows(rows_part, ((inputs, key_grad), (inputs, value_grad)))
    row_copies = start_pairs(lines, rows_part, row_buf)
    sent = forward_pairs(lines, part, buf, copies)
    buf.mine[...] = rounded(finish_scatter(lines, part, buf, copies, sent))
    gathering = start_gather(lines, buf)
    row_sent = forward_pairs(lines, rows_part, row_buf, row_copies)
    relay_gather(lines, buf, gathering)

    tile = math.gcd(inputs.shape[0], 256)
    weights = jnp.concatenate([proj_query[...], proj_key[...], proj_value[...]], axis=1)

    def tokens(i, carry):
        at = pl.ds(pl.multiple_of(i * tile, tile), tile)
        grads = jnp.concatenate([query_grad[at, :], key_grad[at, :], value_grad[at, :]], axis=1)
        back_inputs[at, :] = rounded(times_transpose(grads, weights))
        return carry

    lax.fori_loop(0, inputs.shape[0] // tile, tokens, 0)
    sums = finish_scatter(lines, rows_part, row_buf, row_copies, row_sent)
    h = key_grad.shape[1]
    grad_key[...] = sums[:, :h]
    grad_value[...] = sums[:, h:]
    finish_gather(lines, buf, gathering, total)
    grad_in[...] = adjoint[:h, :] + total[:h, :]
    grad_up[...] = adjoint[h : 2 * h, :] + total[h : 2 * h, :]
    grad_out[...] = (adjoint[2 * h :, :] + total[2 * h :, :]).T


def call(kernel, identity, outs, scratch, *operands):
    vmem = pl.BlockSpec(memory_space=pltpu.VMEM)
    return pl.pallas_call(
        kernel,
        out_shape=[jax.ShapeDtypeStruct(s, d) for s, d in outs],
        in_specs=[vmem] * len(operands),
        out_specs=[vmem] * len(outs),
        scratch_shapes=scratch,
        compiler_params=pltpu.CompilerParams(
            collective_id=identity, has_side_effects=True, vmem_limit_bytes=VMEM_LIMIT
        ),
    )(*operands)


def body(
    n,
    inputs,
    token_rates,
    proj_query,
    proj_key,
    proj_value,
    proj_output,
    fast_in,
    fast_up,
    fast_out,
    cotangent,
):
    bf16, f32 = jnp.bfloat16, jnp.float32
    h, f = fast_in.shape
    width = inputs.shape[1]
    count = 3
    block = (count * h // n, f)
    row_block = (width // n, 2 * h)

    query_rows = rounded(product(inputs, proj_query))
    key_rows = rounded(product(inputs, proj_key))
    value_rows = rounded(product(inputs, proj_value))
    w_in, w_up, w_out = (rounded(fast_in), rounded(fast_up), rounded(fast_out))
    scaled = rounded(token_rates[:, None] * value_rows.astype(f32))
    pre_in = product(key_rows, w_in)
    pre_up = product(key_rows, w_up)
    activation, slope_val, curvature = silu_parts(pre_in)
    hidden = rounded(activation * pre_up)
    upstream = times_transpose(scaled, w_out)
    grad_in_rows = rounded(upstream * pre_up * slope_val)
    grad_up_rows = rounded(upstream * activation)

    def stacked(*terms):
        return jnp.concatenate([rounded(t) for t in terms]).reshape((n,) + block)

    part = stacked(
        token_sum(key_rows, grad_in_rows),
        token_sum(key_rows, grad_up_rows),
        token_sum(scaled, hidden),
    )
    lines = n // PAIR
    exchange = Reduce.scratch(lines, block)
    row_scratch = Scatter.scratch(lines, row_block)
    n_in, n_up, n_out, totals = call(
        functools.partial(forward_kernel, lines, count),
        0,
        [((h, f), bf16), ((h, f), bf16), ((f, h), bf16), ((count * h, f), f32)],
        exchange + [pltpu.VMEM((NS_STEPS + 1, count, h, f), f32)],
        part, fast_in, fast_up, fast_out,
    )

    pre_p = product(query_rows, n_in)
    pre_r = product(query_rows, n_up)
    activation_q, slope_q, _ = silu_parts(pre_p)
    hidden_q = rounded(activation_q * pre_r)
    output_rows = rounded(product(hidden_q, n_out))
    back_output = rounded(times_transpose(cotangent, proj_output))
    back_hidden = times_transpose(back_output, n_out)
    back_p = rounded(back_hidden * pre_r * slope_q)
    back_r = rounded(back_hidden * activation_q)
    query_grad = rounded(times_transpose(back_p, n_in) + times_transpose(back_r, n_up))
    part = stacked(
        token_sum(query_rows, back_p),
        token_sum(query_rows, back_r),
        token_sum(back_output, hidden_q),
    )
    adjoint, back_totals, rows_sum = call(
        functools.partial(backward_kernel, lines, count),
        1,
        [((count * h, f), f32), ((count * h, f), bf16), (row_block, f32)],
        exchange
        + row_scratch
        + [
            pltpu.VMEM((n,) + row_block, bf16),
            pltpu.VMEM((NS_STEPS + 1, count, h, f), f32),
            pltpu.VMEM((NS_STEPS, count, h, h), f32),
            pltpu.VMEM((NS_STEPS, count, h, h), f32),
            pltpu.VMEM((count, h, f), f32),
        ],
        part, inputs, query_grad, cotangent, output_rows, totals,
    )
    grad_query = rows_sum[:, :h]
    grad_output = rows_sum[:, h:].T

    b_in, b_up, b_out = (back_totals[m * h : (m + 1) * h] for m in range(count))
    press_in = product(key_rows, b_in)
    press_up = product(key_rows, b_up)
    back_hid = product(scaled, b_out)
    back_upstream = rounded(press_in * pre_up * slope_val + press_up * activation)
    back_pre_up = rounded(press_in * upstream * slope_val + back_hid * activation)
    back_pre_in = rounded(
        press_in * upstream * pre_up * curvature
        + press_up * upstream * slope_val
        + back_hid * pre_up * slope_val
    )
    back_scaled = times_transpose(hidden, b_out) + product(back_upstream, w_out)
    back_rate = jnp.sum(back_scaled * value_rows.astype(f32), axis=1)
    key_sum = times_transpose(grad_in_rows, b_in) + times_transpose(grad_up_rows, b_up)
    key_sum = key_sum + times_transpose(back_pre_in, w_in) + times_transpose(back_pre_up, w_up)
    key_grad = rounded(key_sum)
    value_grad = rounded(token_rates[:, None] * back_scaled)
    part = stacked(
        token_sum(key_rows, back_pre_in),
        token_sum(key_rows, back_pre_up),
        token_sum(scaled, back_upstream),
    )
    grad_in, grad_up, grad_out, grad_key, grad_value, back_inputs = call(
        functools.partial(final_kernel, lines, count),
        2,
        [
            ((h, f), f32),
            ((h, f), f32),
            ((f, h), f32),
            ((width // n, h), f32),
            ((width // n, h), f32),
            (inputs.shape, bf16),
        ],
        exchange
        + row_scratch
        + [pltpu.VMEM((n,) + row_block, bf16), pltpu.VMEM((count * h, f), f32)],
        part, inputs, query_grad, key_grad, value_grad,
        proj_query, proj_key, proj_value, adjoint,
    )
    return (
        back_inputs,
        back_rate,
        grad_in,
        grad_up,
        grad_out,
        grad_query,
        grad_key,
        grad_value,
        grad_output,
    )


def solution(mesh):
    in_specs = (
        P(("batch", "seq"), None),
        P(("batch", "seq")),
        P(),
        P(),
        P(),
        P(),
        P(),
        P(),
        P(),
        P(("batch", "seq"), None),
    )
    out_specs = (
        P(("batch", "seq"), None),
        P(("batch", "seq")),
        P("batch", None),
        P("batch", None),
        P("batch", None),
        P("seq", "batch"),
        P("seq", "batch"),
        P("seq", "batch"),
        P("batch", "seq"),
    )
    return jax.shard_map(
        functools.partial(body, mesh.shape["seq"]),
        mesh=mesh,
        in_specs=in_specs,
        out_specs=out_specs,
        check_vma=False,
    )
```

```python
import functools
import math

import jax
import jax.numpy as jnp
from jax import lax
from jax.experimental import pallas as pl
from jax.experimental.pallas import tpu as pltpu
from jax.sharding import PartitionSpec as P

NS_STEPS = 5
C1, C3, C5 = 3.4445, -4.775, 2.0315
EPS = 1e-07
MESH = pl.DeviceIdType.MESH
VMEM_LIMIT = 60 * 1024 * 1024
PAIR = 2
PASSES_FWD = 3
PASSES_BWD = 3


def rounded(value):
    return value.astype(jnp.bfloat16)


def product(left, right):
    return jnp.dot(left, right, preferred_element_type=jnp.float32)


def token_sum(left, right):
    return lax.dot_general(
        left, right, (((0,), (0,)), ((), ())), preferred_element_type=jnp.float32
    )


def times_transpose(left, right):
    return lax.dot_general(
        left, right, (((1,), (1,)), ((), ())), preferred_element_type=jnp.float32
    )


def silu_parts(pre_act):
    sigma_val = jax.nn.sigmoid(pre_act)
    activation = pre_act * sigma_val
    slope_val = sigma_val * (1.0 + pre_act * (1.0 - sigma_val))
    curvature = sigma_val * (1.0 - sigma_val) * (2.0 + pre_act * (1.0 - 2.0 * sigma_val))
    return (activation, slope_val, curvature)


def split(value, passes):
    high = rounded(value)
    if passes == 1:
        return (high,)
    return (high, rounded(value - high.astype(jnp.float32)))


def dot_split(left, right, dot):
    if len(left) == 1:
        return dot(left[0], right[0])
    along = 1 if dot is times_transpose else 0
    return dot(
        jnp.concatenate([left[0], left[0], left[1]], axis=1),
        jnp.concatenate([right[0], right[1], right[0]], axis=along),
    )


def ns_start(totals, xs):
    norms = []
    for m, matrix in enumerate(totals):
        norm = jnp.sqrt(jnp.sum(matrix * matrix))
        norms.append(norm)
        xs[0, m] = matrix / (norm + EPS)
    return norms


def ns_forward(first, last, xs, grams, polys, count, passes):
    each = range(count)

    def step(k, carry):
        xparts = [split(xs[k, m], passes) for m in each]
        gram = [dot_split(xparts[m], xparts[m], times_transpose) for m in each]
        gparts = [split(gram[m], passes) for m in each]
        poly = [C3 * gram[m] + C5 * dot_split(gparts[m], gparts[m], product) for m in each]
        pparts = [split(poly[m], passes) for m in each]
        for m in each:
            if grams is not None:
                grams[k, m] = gram[m]
                polys[k, m] = poly[m]
            xs[k + 1, m] = C1 * xs[k, m] + dot_split(pparts[m], xparts[m], product)
        return carry

    lax.fori_loop(first, last, step, 0)


def ns_backward(first, last, xs, grams, polys, grads, count, passes):
    each = range(count)

    def step(i, carry):
        k = NS_STEPS - 1 - i
        gparts = [split(grads[m], passes) for m in each]
        xparts = [split(xs[k, m], passes) for m in each]
        dpoly = [dot_split(gparts[m], xparts[m], times_transpose) for m in each]
        sym = [dpoly[m] + dpoly[m].T for m in each]
        twist = [
            dot_split(split(sym[m], passes), split(grams[k, m], passes), product) for m in each
        ]
        weight = [C3 * sym[m] + C5 * (twist[m] + twist[m].T) for m in each]
        for m in each:
            grads[m] = (
                C1 * grads[m]
                + dot_split(split(polys[k, m], passes), gparts[m], product)
                + dot_split(split(weight[m], passes), xparts[m], product)
            )
        return carry

    lax.fori_loop(first, last, step, 0)


def ns_finish(totals, norms, grads, count):
    out = []
    for m in range(count):
        shifted = norms[m] + EPS
        dot_all = jnp.sum(grads[m] * totals[m])
        out.append(grads[m] / shifted - totals[m] * (dot_all / (norms[m] * shifted * shifted)))
    return out


def place():
    me = lax.axis_index("seq")
    return me // PAIR, me % PAIR


def remote(src, dst, send, recv, device):
    copy = pltpu.make_async_remote_copy(
        src_ref=src,
        dst_ref=dst,
        send_sem=send,
        recv_sem=recv,
        device_id={"seq": device},
        device_id_type=MESH,
    )
    copy.start()
    return copy


def line_peer(lines, d):
    line, side = place()
    return lax.rem(line + d, lines) * PAIR + side


def partner():
    line, side = place()
    return line * PAIR + (1 - side)


def greet(lines):
    barrier = pltpu.get_barrier_semaphore()
    for peer in [partner()] + [line_peer(lines, d) for d in range(1, lines)]:
        pl.semaphore_signal(barrier, inc=1, device_id={"seq": peer}, device_id_type=MESH)
    pl.semaphore_wait(barrier, lines)


def start_pairs(lines, src, buf):
    line, side = place()
    copies = []
    for d in list(range(1, lines)) + [0]:
        to = lax.rem(line + d, lines)
        copies.append(
            remote(
                src.at[to * PAIR + (1 - side)],
                buf.paired.at[d],
                buf.sems.at[0, d],
                buf.sems.at[1, d],
                partner(),
            )
        )
    return copies


def forward_pairs(lines, src, buf, copies, first=1, last=None):
    line, side = place()
    sent = []
    for d in range(lines if last is None else last)[first:]:
        copy = copies[d - 1]
        to = lax.rem(line + d, lines)
        copy.wait()
        buf.middle[d] = rounded(
            src[to * PAIR + side].astype(jnp.float32) + buf.paired[d].astype(jnp.float32)
        )
        sent.append(
            remote(
                buf.middle.at[d],
                buf.lined.at[d],
                buf.sems.at[2, d],
                buf.sems.at[3, d],
                to * PAIR + side,
            )
        )
    return sent


def finish_scatter(lines, src, buf, copies, sent):
    copies[-1].wait()
    total = src[lax.axis_index("seq")].astype(jnp.float32) + buf.paired[0].astype(jnp.float32)
    for d, copy in zip(range(1, lines), sent):
        copy.wait()
        total = total + buf.lined[d].astype(jnp.float32)
    return total


def start_gather(lines, buf):
    out = []
    for d in range(1, lines):
        out.append(
            remote(
                buf.mine,
                buf.gathered.at[d],
                buf.sems.at[4, d],
                buf.sems.at[5, d],
                line_peer(lines, d),
            )
        )
    across = remote(buf.mine, buf.crossed.at[0], buf.sems.at[6, 0], buf.sems.at[7, 0], partner())
    return out, [across]


def relay_gather(lines, buf, copies):
    out, across = copies
    for d in range(1, lines):
        out[d - 1].wait()
        across.append(
            remote(
                buf.gathered.at[d],
                buf.crossed.at[d],
                buf.sems.at[6, d],
                buf.sems.at[7, d],
                partner(),
            )
        )


def finish_gather(lines, buf, copies, full):
    line, side = place()
    rows = buf.mine.shape[0]
    across = copies[1]

    def put(owner, block):
        full[pl.ds(pl.multiple_of(owner * rows, rows), rows), :] = block.astype(jnp.float32)

    put(line * PAIR + side, buf.mine[...])
    for d in range(1, lines):
        put(lax.rem(line - d + lines, lines) * PAIR + side, buf.gathered[d])
    for d in range(lines):
        across[d].wait()
        put(lax.rem(line - d + lines, lines) * PAIR + (1 - side), buf.crossed[d])


class Scatter:
    def __init__(self, paired, middle, lined, sems):
        self.paired, self.middle, self.lined, self.sems = paired, middle, lined, sems

    @staticmethod
    def scratch(lines, block):
        slots = pltpu.VMEM((lines,) + block, jnp.bfloat16)
        return [slots, slots, slots, pltpu.SemaphoreType.DMA((4, lines))]


class Reduce(Scatter):
    def __init__(self, paired, middle, lined, mine, gathered, crossed, sems):
        super().__init__(paired, middle, lined, sems)
        self.mine, self.gathered, self.crossed = mine, gathered, crossed

    @staticmethod
    def scratch(lines, block):
        slots = pltpu.VMEM((lines,) + block, jnp.bfloat16)
        one = pltpu.VMEM(block, jnp.bfloat16)
        return [slots, slots, slots, one, slots, slots, pltpu.SemaphoreType.DMA((8, lines))]


def forward_kernel(
    lines, count, part, fast_in, fast_up, fast_out, inputs, proj_query, cotangent, proj_output,
    n_in, n_up, n_out, total_out, query_rows, back_output, *scratch
):
    buf, xs = Reduce(*scratch[:7]), scratch[7]
    greet(lines)
    copies = start_pairs(lines, part, buf)
    query_rows[...] = rounded(product(inputs[...], proj_query[...]))
    back_output[...] = rounded(times_transpose(cotangent[...], proj_output[...]))
    sent = forward_pairs(lines, part, buf, copies)
    buf.mine[...] = rounded(finish_scatter(lines, part, buf, copies, sent))
    gathering = start_gather(lines, buf)
    relay_gather(lines, buf, gathering)
    finish_gather(lines, buf, gathering, total_out)
    h = total_out.shape[0] // count
    totals = [total_out[m * h : (m + 1) * h, :] for m in range(count)]
    ns_start(totals, xs)
    ns_forward(0, NS_STEPS, xs, None, None, count, PASSES_FWD)
    n_in[...] = rounded(fast_in[...] + xs[NS_STEPS, 0])
    n_up[...] = rounded(fast_up[...] + xs[NS_STEPS, 1])
    n_out[...] = rounded(fast_out[...] + xs[NS_STEPS, 2].T)


def fill_rows(rows_part, pairs):
    n, rows = rows_part.shape[:2]
    at = 0
    for left, right in pairs:
        total = token_sum(left[...], right[...])
        wide = total.shape[1]
        for j in range(n):
            rows_part[j, :, at : at + wide] = rounded(total[j * rows : (j + 1) * rows, :])
        at += wide


def backward_kernel(
    lines, count, part, inputs, query_grad, cotangent, output_rows, total_ref,
    adjoint_out, back_out, rows_out, *scratch
):
    buf, row_buf = Reduce(*scratch[:7]), Scatter(*scratch[7:11])
    rows_part, xs, grams, polys, grads = scratch[11:]
    greet(lines)
    copies = start_pairs(lines, part, buf)
    h = total_ref.shape[0] // count
    totals = [total_ref[m * h : (m + 1) * h, :] for m in range(count)]
    norms = ns_start(totals, xs)
    fill_rows(rows_part, ((inputs, query_grad), (cotangent, output_rows)))
    sent = forward_pairs(lines, part, buf, copies, 1, lines - 1)
    ns_forward(0, NS_STEPS - 4, xs, grams, polys, count, PASSES_FWD)
    sent += forward_pairs(lines, part, buf, copies, lines - 1)
    ns_forward(NS_STEPS - 4, NS_STEPS - 2, xs, grams, polys, count, PASSES_FWD)
    buf.mine[...] = rounded(finish_scatter(lines, part, buf, copies, sent))
    gathering = start_gather(lines, buf)
    ns_forward(NS_STEPS - 2, NS_STEPS - 1, xs, grams, polys, count, PASSES_FWD)
    relay_gather(lines, buf, gathering)
    ns_forward(NS_STEPS - 1, NS_STEPS, xs, grams, polys, count, PASSES_FWD)
    finish_gather(lines, buf, gathering, adjoint_out)
    copies = start_pairs(lines, rows_part, row_buf)
    for m in range(count):
        grads[m] = adjoint_out[m * h : (m + 1) * h, :]
    ns_backward(0, NS_STEPS - 2, xs, grams, polys, grads, count, PASSES_BWD)
    sent = forward_pairs(lines, rows_part, row_buf, copies)
    ns_backward(NS_STEPS - 2, NS_STEPS, xs, grams, polys, grads, count, PASSES_BWD)
    result = ns_finish(totals, norms, grads, count)
    for m in range(count):
        back_out[m * h : (m + 1) * h, :] = rounded(result[m])
    rows_out[...] = finish_scatter(lines, rows_part, row_buf, copies, sent)


def final_kernel(
    lines, count, part, inputs, query_grad, key_grad, value_grad,
    proj_query, proj_key, proj_value, adjoint,
    grad_in, grad_up, grad_out, grad_key, grad_value, back_inputs, *scratch
):
    buf, row_buf = Reduce(*scratch[:7]), Scatter(*scratch[7:11])
    rows_part, total = scratch[11:]
    greet(lines)
    copies = start_pairs(lines, part, buf)
    fill_rows(rows_part, ((inputs, key_grad), (inputs, value_grad)))
    row_copies = start_pairs(lines, rows_part, row_buf)
    sent = forward_pairs(lines, part, buf, copies)
    buf.mine[...] = rounded(finish_scatter(lines, part, buf, copies, sent))
    gathering = start_gather(lines, buf)
    row_sent = forward_pairs(lines, rows_part, row_buf, row_copies)
    relay_gather(lines, buf, gathering)

    tile = math.gcd(inputs.shape[0], 256)
    weights = jnp.concatenate([proj_query[...], proj_key[...], proj_value[...]], axis=1)

    def tokens(i, carry):
        at = pl.ds(pl.multiple_of(i * tile, tile), tile)
        grads = jnp.concatenate([query_grad[at, :], key_grad[at, :], value_grad[at, :]], axis=1)
        back_inputs[at, :] = rounded(times_transpose(grads, weights))
        return carry

    lax.fori_loop(0, inputs.shape[0] // tile, tokens, 0)
    sums = finish_scatter(lines, rows_part, row_buf, row_copies, row_sent)
    h = key_grad.shape[1]
    grad_key[...] = sums[:, :h]
    grad_value[...] = sums[:, h:]
    finish_gather(lines, buf, gathering, total)
    grad_in[...] = adjoint[:h, :] + total[:h, :]
    grad_up[...] = adjoint[h : 2 * h, :] + total[h : 2 * h, :]
    grad_out[...] = (adjoint[2 * h :, :] + total[2 * h :, :]).T


def call(kernel, identity, outs, scratch, *operands):
    vmem = pl.BlockSpec(memory_space=pltpu.VMEM)
    return pl.pallas_call(
        kernel,
        out_shape=[jax.ShapeDtypeStruct(s, d) for s, d in outs],
        in_specs=[vmem] * len(operands),
        out_specs=[vmem] * len(outs),
        scratch_shapes=scratch,
        compiler_params=pltpu.CompilerParams(
            collective_id=identity, has_side_effects=True, vmem_limit_bytes=VMEM_LIMIT
        ),
    )(*operands)


def body(
    n,
    inputs,
    token_rates,
    proj_query,
    proj_key,
    proj_value,
    proj_output,
    fast_in,
    fast_up,
    fast_out,
    cotangent,
):
    bf16, f32 = jnp.bfloat16, jnp.float32
    h, f = fast_in.shape
    width = inputs.shape[1]
    count = 3
    block = (count * h // n, f)
    row_block = (width // n, 2 * h)

    key_rows = rounded(product(inputs, proj_key))
    value_rows = rounded(product(inputs, proj_value))
    w_in, w_up, w_out = (rounded(fast_in), rounded(fast_up), rounded(fast_out))
    scaled = rounded(token_rates[:, None] * value_rows.astype(f32))
    pre_in = product(key_rows, w_in)
    pre_up = product(key_rows, w_up)
    activation, slope_val, curvature = silu_parts(pre_in)
    hidden = rounded(activation * pre_up)
    upstream = times_transpose(scaled, w_out)
    grad_in_rows = rounded(upstream * pre_up * slope_val)
    grad_up_rows = rounded(upstream * activation)

    def stacked(*terms):
        return jnp.concatenate([rounded(t) for t in terms]).reshape((n,) + block)

    part = stacked(
        token_sum(key_rows, grad_in_rows),
        token_sum(key_rows, grad_up_rows),
        token_sum(scaled, hidden),
    )
    lines = n // PAIR
    exchange = Reduce.scratch(lines, block)
    row_scratch = Scatter.scratch(lines, row_block)
    n_in, n_up, n_out, totals, query_rows, back_output = call(
        functools.partial(forward_kernel, lines, count),
        0,
        [
            ((h, f), bf16),
            ((h, f), bf16),
            ((f, h), bf16),
            ((count * h, f), f32),
            ((inputs.shape[0], h), bf16),
            ((inputs.shape[0], h), bf16),
        ],
        exchange + [pltpu.VMEM((NS_STEPS + 1, count, h, f), f32)],
        part, fast_in, fast_up, fast_out, inputs, proj_query, cotangent, proj_output,
    )

    pre_p = product(query_rows, n_in)
    pre_r = product(query_rows, n_up)
    activation_q, slope_q, _ = silu_parts(pre_p)
    hidden_q = rounded(activation_q * pre_r)
    output_rows = rounded(product(hidden_q, n_out))
    back_hidden = times_transpose(back_output, n_out)
    back_p = rounded(back_hidden * pre_r * slope_q)
    back_r = rounded(back_hidden * activation_q)
    query_grad = rounded(times_transpose(back_p, n_in) + times_transpose(back_r, n_up))
    part = stacked(
        token_sum(query_rows, back_p),
        token_sum(query_rows, back_r),
        token_sum(back_output, hidden_q),
    )
    adjoint, back_totals, rows_sum = call(
        functools.partial(backward_kernel, lines, count),
        1,
        [((count * h, f), f32), ((count * h, f), bf16), (row_block, f32)],
        exchange
        + row_scratch
        + [
            pltpu.VMEM((n,) + row_block, bf16),
            pltpu.VMEM((NS_STEPS + 1, count, h, f), f32),
            pltpu.VMEM((NS_STEPS, count, h, h), f32),
            pltpu.VMEM((NS_STEPS, count, h, h), f32),
            pltpu.VMEM((count, h, f), f32),
        ],
        part, inputs, query_grad, cotangent, output_rows, totals,
    )
    grad_query = rows_sum[:, :h]
    grad_output = rows_sum[:, h:].T

    b_in, b_up, b_out = (back_totals[m * h : (m + 1) * h] for m in range(count))
    press_in = product(key_rows, b_in)
    press_up = product(key_rows, b_up)
    back_hid = product(scaled, b_out)
    back_upstream = rounded(press_in * pre_up * slope_val + press_up * activation)
    back_pre_up = rounded(press_in * upstream * slope_val + back_hid * activation)
    back_pre_in = rounded(
        press_in * upstream * pre_up * curvature
        + press_up * upstream * slope_val
        + back_hid * pre_up * slope_val
    )
    back_scaled = times_transpose(hidden, b_out) + product(back_upstream, w_out)
    back_rate = jnp.sum(back_scaled * value_rows.astype(f32), axis=1)
    key_sum = times_transpose(grad_in_rows, b_in) + times_transpose(grad_up_rows, b_up)
    key_sum = key_sum + times_transpose(back_pre_in, w_in) + times_transpose(back_pre_up, w_up)
    key_grad = rounded(key_sum)
    value_grad = rounded(token_rates[:, None] * back_scaled)
    part = stacked(
        token_sum(key_rows, back_pre_in),
        token_sum(key_rows, back_pre_up),
        token_sum(scaled, back_upstream),
    )
    grad_in, grad_up, grad_out, grad_key, grad_value, back_inputs = call(
        functools.partial(final_kernel, lines, count),
        2,
        [
            ((h, f), f32),
            ((h, f), f32),
            ((f, h), f32),
            ((width // n, h), f32),
            ((width // n, h), f32),
            (inputs.shape, bf16),
        ],
        exchange
        + row_scratch
        + [pltpu.VMEM((n,) + row_block, bf16), pltpu.VMEM((count * h, f), f32)],
        part, inputs, query_grad, key_grad, value_grad,
        proj_query, proj_key, proj_value, adjoint,
    )
    return (
        back_inputs,
        back_rate,
        grad_in,
        grad_up,
        grad_out,
        grad_query,
        grad_key,
        grad_value,
        grad_output,
    )


def solution(mesh):
    in_specs = (
        P(("batch", "seq"), None),
        P(("batch", "seq")),
        P(),
        P(),
        P(),
        P(),
        P(),
        P(),
        P(),
        P(("batch", "seq"), None),
    )
    out_specs = (
        P(("batch", "seq"), None),
        P(("batch", "seq")),
        P("batch", None),
        P("batch", None),
        P("batch", None),
        P("seq", "batch"),
        P("seq", "batch"),
        P("seq", "batch"),
        P("batch", "seq"),
    )
    return jax.shard_map(
        functools.partial(body, mesh.shape["seq"]),
        mesh=mesh,
        in_specs=in_specs,
        out_specs=out_specs,
        check_vma=False,
    )
```
